32 devices in a mesh: band: 16 (over z, x, core), lev: 2 (over y).
Axes of the slice: x: 2, y: 2, z: 4, core: 2. Of those that a mesh axis runs over, the one named last changes fastest.
Arguments:
- field_grid: float32 [3, 8, 384, 2, 1536], P(None, 'lev', 'band'), may hold values from -6 to 6
- increment: float32 [3, 8, 384, 2, 1536], P(None, 'lev', 'band'), may hold values from -6 to 6
- points: int32 [384], P('band'), may hold values from 16 to 1536, as said below
- weights: float32 [384], replicated, may hold values from 0.0013020834 to 0.0052083335
- pair_slot: int32 [384], replicated, may hold values from 0 to 383, each once
- legendre: float32 [384, 384, 769], P(('band', 'lev')), may hold values from -6 to 6
- strength: float32 [3, 8], replicated, may hold values from 1 to 16
Outputs:
- stepped: float32 [3, 8, 384, 2, 1536], P(None, 'lev', 'band')
The draws below stay inside these ranges and needn't reach their ends.
Inputs may be any that keep to these rules, and one draw needn't show every extreme that they name: points[j] lies within 32 of 16 + 1520 * j // 383, kept within 16 to 1536; the last latitude pair has 1536 cells. `pair_slot`: A permutation of 0 to 383; slot s is held by the device of joint band+lev index s // 12, at place s % 12, which holds legendre[s].
All inputs are finite; a program needn't handle non-finite values.
Results may differ from the reference program's by a relative error of at most 0.0003.
Values sent between devices are 32-bit elements; how exact they have to be, the bound alone decides.
No kernel may reach another device: no remote copies, remote signals or barrier semaphores. Data moves between devices by JAX's collectives and lax.ppermute only.
A program may use at most 320 MiB of HBM per device.

```python
import math
import jax
import jax.numpy as jnp
from jax import lax

WAVES = 768
FIELDS = 3
HALF = 384
NLON = 1536
LEVELS = 8


def draw_points(key, part):
    pair_index = lax.iota(jnp.int32, HALF)
    smooth_count = 16 + (2 * WAVES - 16) * pair_index // (HALF - 1)
    jitter = jax.random.randint(key, (HALF,), -32, 33)
    counts = jnp.clip(smooth_count + jitter, 16, 2 * WAVES)
    return jnp.where(pair_index == HALF - 1, 2 * WAVES, counts).astype(jnp.int32)


def levels(own_key, dims, cuts, least, high):
    level, own = 1.0, jax.random.fold_in(own_key, 6)
    for position, shards_of in cuts:
        draws = jnp.exp(jax.random.uniform(jax.random.fold_in(own, position), (shards_of,), jnp.float32, least / len(cuts), high / len(cuts)))
        level = level * jnp.repeat(draws, dims[position] // shards_of).reshape([-1 if axis == position else 1 for axis in range(len(dims))])
    return level


def normal_values(rng, shape, spread, bound, cuts=(), kind=jnp.bfloat16):
    entries = jax.random.normal(rng, shape, jnp.float32) * spread
    if len(cuts) > 0:
        entries = levels(rng, shape, cuts, -0.22, 0.18) * entries
    return jnp.clip(entries, min=-bound, max=bound).astype(kind)


def setup_inputs(seed: int = 0) -> dict:
    arg_keys = jax.random.split(jax.random.key(seed), 8)
    return {
        "field_grid": normal_values(arg_keys[0], (FIELDS, LEVELS, HALF, 2, NLON), 1.0, 6.0, ((1, 2), (2, 16)), jnp.float32),
        "increment": normal_values(arg_keys[1], (FIELDS, LEVELS, HALF, 2, NLON), 1.0, 6.0, ((1, 2), (2, 16)), jnp.float32),
        "points": draw_points(jax.random.fold_in(arg_keys[7], 71), 0),
        "weights": jnp.clip(jnp.exp(jax.random.uniform(arg_keys[3], (HALF,), jnp.float32, math.log(0.0013020834), math.log(0.0052083335))), 0.0013020834, 0.0052083335),
        "pair_slot": jax.random.permutation(arg_keys[4], HALF).astype(jnp.int32),
        "legendre": normal_values(arg_keys[5], (HALF, HALF, WAVES + 1), 1.0, 6.0, ((0, 32),), jnp.float32),
        "strength": jnp.clip(jnp.exp(jax.random.uniform(arg_keys[6], (FIELDS, LEVELS), jnp.float32, math.log(1.0), math.log(16.0))), 1.0, 16.0),
    }


TWO_PI = 2.0 * math.pi


def dft_basis(count):
    places = lax.iota(jnp.int32, NLON)
    orders = lax.iota(jnp.int32, WAVES)
    turns = (places[:, None] * orders[None, :]) % count
    angle = turns.astype(jnp.float32) * (TWO_PI / count.astype(jnp.float32))
    live = (places[:, None] < count) & (orders[None, :] <= (count - 1) // 2)
    cosines = jnp.where(live, jnp.cos(angle), 0.0)
    sines = jnp.where(live, -jnp.sin(angle), 0.0)
    return jnp.concatenate([cosines, sines], axis=1)


def reference(field_grid, increment, points, weights, pair_slot, legendre, strength):
    summed = field_grid + increment
    row_count = FIELDS * LEVELS * 2
    by_pair = jnp.moveaxis(summed, 2, 0).reshape(HALF, row_count, NLON)

    def forward(item):
        block, count = item
        product = jnp.dot(block, dft_basis(count), precision=lax.Precision.HIGHEST)
        return product / count.astype(jnp.float32)

    spectra = lax.map(forward, (by_pair, points))
    spectra = spectra.reshape(HALF, FIELDS * LEVELS, 2, 2, WAVES)
    columns = lax.iota(jnp.int32, WAVES + 1)
    degree_top = float((WAVES - 1) * WAVES)
    damping_rate = strength.reshape(FIELDS * LEVELS)

    def per_pair(lower_wave):
        table = lax.dynamic_index_in_dim(legendre, pair_slot[lower_wave], 0, keepdims=False)
        higher_wave = WAVES - 1 - lower_wave
        first = lax.dynamic_index_in_dim(spectra, lower_wave, 4, keepdims=False)
        second = lax.dynamic_index_in_dim(spectra, higher_wave, 4, keepdims=False)
        second_member = columns >= WAVES - lower_wave
        degree = jnp.where(second_member, columns - 1, lower_wave + columns)
        wave_of_column = jnp.where(second_member, higher_wave, lower_wave)
        parity = jnp.where((degree - wave_of_column) % 2 == 0, 1.0, -1.0)
        first_weighted = (first * weights[:, None, None, None]).reshape(HALF, -1)
        second_weighted = (second * weights[:, None, None, None]).reshape(HALF, -1)
        part_first = jnp.dot(table.T, first_weighted, precision=lax.Precision.HIGHEST)
        part_second = jnp.dot(table.T, second_weighted, precision=lax.Precision.HIGHEST)
        part_first = part_first.reshape(WAVES + 1, FIELDS * LEVELS, 2, 2)
        part_second = part_second.reshape(WAVES + 1, FIELDS * LEVELS, 2, 2)
        chosen = jnp.where(second_member[:, None, None, None], part_second, part_first)
        coefficients = chosen[:, :, 0, :] + parity[:, None, None] * chosen[:, :, 1, :]
        degree_real = degree.astype(jnp.float32)
        degree_ratio = degree_real * (degree_real + 1.0) / degree_top
        damping = 1.0 / (1.0 + damping_rate[None, :] * (degree_ratio * degree_ratio)[:, None])
        damped = coefficients * damping[:, :, None]
        lower_part = jnp.where(second_member[:, None, None], 0.0, damped)
        upper_part = jnp.where(second_member[:, None, None], damped, 0.0)
        stacked = jnp.stack([lower_part, lower_part * parity[:, None, None],
                             upper_part, upper_part * parity[:, None, None]], axis=1)
        returned = jnp.dot(table, stacked.reshape(WAVES + 1, -1), precision=lax.Precision.HIGHEST)
        returned = returned.reshape(HALF, 2, 2, FIELDS * LEVELS, 2)
        return returned[:, 0], returned[:, 1]

    first_back, second_back = lax.map(per_pair, lax.iota(jnp.int32, HALF))
    by_wave = jnp.concatenate([first_back, second_back[::-1]], axis=0)
    spectral_rows = jnp.transpose(by_wave, (1, 3, 2, 4, 0)).reshape(HALF, row_count, 2 * WAVES)
    doubling = jnp.where(lax.iota(jnp.int32, 2 * WAVES) % WAVES == 0, 1.0, 2.0)

    def inverse(item):
        block, count = item
        return jnp.dot(block * doubling[None, :], dft_basis(count).T, precision=lax.Precision.HIGHEST)

    grid_rows = lax.map(inverse, (spectral_rows, points))
    grid_rows = grid_rows.reshape(HALF, FIELDS, LEVELS, 2, NLON)
    return jnp.moveaxis(grid_rows, 0, 2)
```

```python
import math

import jax
import jax.numpy as jnp
from jax import lax
from jax.sharding import PartitionSpec as P

INNER = 256


def turn_cos_sin(product, counts):
    inverse = 1.0 / counts
    whole = jnp.round(product * inverse)
    half = (product - whole * counts) * inverse * math.pi
    square = half * half
    sine = jnp.full_like(square, -1.0 / math.factorial(11))
    for order, sign in ((9, 1.0), (7, -1.0), (5, 1.0), (3, -1.0), (1, 1.0)):
        sine = sine * square + sign / math.factorial(order)
    sine = sine * half
    cosine = jnp.full_like(square, 1.0 / math.factorial(12))
    for order, sign in ((10, -1.0), (8, 1.0), (6, -1.0), (4, 1.0), (2, -1.0), (0, 1.0)):
        cosine = cosine * square + sign / math.factorial(order)
    return 1.0 - 2.0 * sine * sine, 2.0 * sine * cosine


def body(field_grid, increment, points, weights, pair_slot, legendre, strength):
    band_count = lax.axis_size("band")
    level_groups = lax.axis_size("lev")
    fields, local_levels, band_pairs, _, length = field_grid.shape
    wavecount = length // 2
    pair_total = wavecount // 2
    slot_count = legendre.shape[0]
    outer = length // INNER
    stack = fields * local_levels
    rows = 2 * stack
    width = 2 * rows
    high = lax.Precision.HIGH

    slot_ranks = lax.iota(jnp.int32, pair_total)
    matches = pair_slot[None, :] == slot_ranks[:, None]
    pair_of_slot = jnp.sum(jnp.where(matches, slot_ranks[None, :], 0), axis=1)
    wave_order = jnp.stack([pair_of_slot, wavecount - 1 - pair_of_slot], axis=1).reshape(wavecount)
    waves = wave_order.astype(jnp.float32)
    counts = points.astype(jnp.float32)
    fine = lax.iota(jnp.int32, INNER).astype(jnp.float32)
    coarse = (lax.iota(jnp.int32, outer) * INNER).astype(jnp.float32)
    fine_cos, fine_sin = turn_cos_sin(
        fine[None, :, None] * waves[None, None, :], counts[:, None, None]
    )
    turn_cos, turn_sin = turn_cos_sin(
        coarse[None, :, None] * waves[None, None, :], counts[:, None, None]
    )
    table_cos, table_neg = lax.optimization_barrier((fine_cos, -fine_sin))
    live_wave = wave_order[None, :] <= ((points - 1) // 2)[:, None]
    own_weights = lax.dynamic_slice_in_dim(
        weights, lax.axis_index("band") * band_pairs, band_pairs
    )
    ahead = jnp.where(live_wave, (own_weights / counts)[:, None], 0.0)[:, None, :]
    behind = jnp.where(live_wave, jnp.where(wave_order == 0, 1.0, 2.0)[None, :], 0.0)[:, None, :]
    ahead_cos, ahead_sin = turn_cos * ahead, turn_sin * ahead
    behind_cos, behind_sin = turn_cos * behind, turn_sin * behind
    places = lax.iota(jnp.int32, length).reshape(outer, INNER)
    live_cell = places[None, :, :] < points[:, None, None]

    summed = (field_grid + increment).reshape(stack, band_pairs, 2, outer, INNER)
    north, south = summed[:, :, 0], summed[:, :, 1]
    folded = jnp.stack([north + south, north - south], axis=0)
    folded = jnp.transpose(folded, (2, 3, 0, 1, 4)).reshape(band_pairs, outer, rows, INNER)
    folded = jnp.where(live_cell[:, :, None, :], folded, 0.0)
    folded = folded.reshape(band_pairs, outer * rows, INNER)
    part_cos = jnp.einsum("pyb,pbm->pym", folded, table_cos, precision=high)
    part_neg = jnp.einsum("pyb,pbm->pym", folded, table_neg, precision=high)
    part_cos = part_cos.reshape(band_pairs, outer, rows, wavecount)
    part_neg = part_neg.reshape(band_pairs, outer, rows, wavecount)
    real = jnp.sum(
        ahead_cos[:, :, None, :] * part_cos + ahead_sin[:, :, None, :] * part_neg, axis=1
    )
    imag = jnp.sum(
        ahead_cos[:, :, None, :] * part_neg - ahead_sin[:, :, None, :] * part_cos, axis=1
    )
    spectra = jnp.stack([real, imag], axis=1).reshape(band_pairs * width, wavecount)
    outgoing = spectra.T.reshape(
        band_count * level_groups, 2 * slot_count, band_pairs * width
    )
    arrived = lax.all_to_all(outgoing, ("band", "lev"), split_axis=0, concat_axis=0, tiled=True)
    arrived = arrived.reshape(band_count, level_groups, slot_count, 2, band_pairs, width)
    arrived = jnp.transpose(arrived, (2, 0, 4, 3, 1, 5))
    lat_count = band_count * band_pairs
    row_width = 2 * level_groups * width
    arrived = arrived.reshape(slot_count, lat_count, row_width)

    own_slots = lax.axis_index(("band", "lev")) * slot_count + lax.iota(jnp.int32, slot_count)
    lower_wave = jnp.take(pair_of_slot, own_slots)
    columns = lax.iota(jnp.int32, wavecount + 1)
    second_member = columns[None, :] >= (wavecount - lower_wave)[:, None]
    degree = jnp.where(second_member, columns[None, :] - 1, lower_wave[:, None] + columns[None, :])
    wave_of_column = jnp.where(
        second_member, wavecount - 1 - lower_wave[:, None], lower_wave[:, None]
    )
    odd = (degree - wave_of_column) % 2
    degree_real = degree.astype(jnp.float32)
    degree_ratio = degree_real * (degree_real + 1.0) / float((wavecount - 1) * wavecount)
    lane = lax.iota(jnp.int32, row_width)
    lane_group = lane // (level_groups * width) * 2 + lane // stack % 2
    column_group = second_member.astype(jnp.int32) * 2 + odd
    own = strength.reshape(fields, level_groups, local_levels)
    rate = jnp.moveaxis(own, 1, 0).reshape(1, level_groups, 1, stack)
    rate = jnp.broadcast_to(rate, (2, level_groups, 4, stack)).reshape(row_width)
    damping = 1.0 / (1.0 + rate[None, None, :] * (degree_ratio * degree_ratio)[:, :, None])
    damping = jnp.where(column_group[:, :, None] == lane_group[None, None, :], damping, 0.0)
    analysed = jnp.einsum("sjc,sjr->scr", legendre, arrived, precision=high)
    returned = jnp.einsum("sjc,scr->sjr", legendre, analysed * damping, precision=high)

    leaving = returned.reshape(slot_count, band_count, band_pairs, 2, level_groups, width)
    leaving = jnp.transpose(leaving, (1, 4, 0, 3, 2, 5)).reshape(
        band_count * level_groups, 2 * slot_count, band_pairs * width
    )
    home = lax.all_to_all(leaving, ("band", "lev"), split_axis=0, concat_axis=0, tiled=True)
    home = home.reshape(wavecount, band_pairs * width).T.reshape(band_pairs, 2, rows, wavecount)
    real, imag = home[:, 0][:, None], home[:, 1][:, None]
    turned_real = real * behind_cos[:, :, None, :] - imag * behind_sin[:, :, None, :]
    turned_imag = real * behind_sin[:, :, None, :] + imag * behind_cos[:, :, None, :]
    turned_real = turned_real.reshape(band_pairs, outer * rows, wavecount)
    turned_imag = turned_imag.reshape(band_pairs, outer * rows, wavecount)
    cells = jnp.einsum("pym,pbm->pyb", turned_real, table_cos, precision=high)
    cells = cells + jnp.einsum("pym,pbm->pyb", turned_imag, table_neg, precision=high)
    cells = cells.reshape(band_pairs, outer, rows, INNER)
    cells = jnp.where(live_cell[:, :, None, :], cells, 0.0)
    cells = cells.reshape(band_pairs, outer, 2, stack, INNER)
    even, uneven = cells[:, :, 0], cells[:, :, 1]
    stepped = jnp.stack([even + uneven, even - uneven], axis=0)
    stepped = jnp.transpose(stepped, (3, 1, 0, 2, 4))
    return stepped.reshape(fields, local_levels, band_pairs, 2, length)


def solution(mesh):
    return jax.shard_map(
        body,
        mesh=mesh,
        in_specs=(
            P(None, "lev", "band", None, None),
            P(None, "lev", "band", None, None),
            P("band"),
            P(),
            P(),
            P(("band", "lev"), None, None),
            P(),
        ),
        out_specs=P(None, "lev", "band", None, None),
        check_vma=False,
    )
```

```python
import math

import jax
import jax.numpy as jnp
from jax import lax
from jax.sharding import PartitionSpec as P

INNER = 256


def turn_cos_sin(product, counts):
    inverse = 1.0 / counts
    whole = jnp.round(product * inverse)
    half = (product - whole * counts) * inverse * math.pi
    square = half * half
    sine = jnp.full_like(square, -1.0 / math.factorial(11))
    for order, sign in ((9, 1.0), (7, -1.0), (5, 1.0), (3, -1.0), (1, 1.0)):
        sine = sine * square + sign / math.factorial(order)
    sine = sine * half
    cosine = jnp.full_like(square, 1.0 / math.factorial(12))
    for order, sign in ((10, -1.0), (8, 1.0), (6, -1.0), (4, 1.0), (2, -1.0), (0, 1.0)):
        cosine = cosine * square + sign / math.factorial(order)
    return 1.0 - 2.0 * sine * sine, 2.0 * sine * cosine


def body(field_grid, increment, points, weights, pair_slot, legendre, strength):
    band_count = lax.axis_size("band")
    level_groups = lax.axis_size("lev")
    fields, local_levels, band_pairs, _, length = field_grid.shape
    wavecount = length // 2
    pair_total = wavecount // 2
    slot_count = legendre.shape[0]
    outer = length // INNER
    stack = fields * local_levels
    rows = 2 * stack
    width = 2 * rows
    high = lax.Precision.HIGH

    slot_ranks = lax.iota(jnp.int32, pair_total)
    matches = pair_slot[None, :] == slot_ranks[:, None]
    pair_of_slot = jnp.sum(jnp.where(matches, slot_ranks[None, :], 0), axis=1)
    wave_order = jnp.stack([pair_of_slot, wavecount - 1 - pair_of_slot], axis=1).reshape(wavecount)
    waves = wave_order.astype(jnp.float32)
    counts = points.astype(jnp.float32)
    fine = lax.iota(jnp.int32, INNER).astype(jnp.float32)
    coarse = (lax.iota(jnp.int32, outer) * INNER).astype(jnp.float32)
    fine_cos, fine_sin = turn_cos_sin(
        fine[None, :, None] * waves[None, None, :], counts[:, None, None]
    )
    turn_cos, turn_sin = turn_cos_sin(
        coarse[None, :, None] * waves[None, None, :], counts[:, None, None]
    )
    table_cos, table_neg = lax.optimization_barrier((fine_cos, -fine_sin))
    live_wave = wave_order[None, :] <= ((points - 1) // 2)[:, None]
    own_weights = lax.dynamic_slice_in_dim(
        weights, lax.axis_index("band") * band_pairs, band_pairs
    )
    ahead = jnp.where(live_wave, (own_weights / counts)[:, None], 0.0)[:, None, :]
    behind = jnp.where(live_wave, jnp.where(wave_order == 0, 1.0, 2.0)[None, :], 0.0)[:, None, :]
    ahead_cos, ahead_sin = turn_cos * ahead, turn_sin * ahead
    behind_cos, behind_sin = turn_cos * behind, turn_sin * behind
    places = lax.iota(jnp.int32, length).reshape(outer, INNER)
    live_cell = places[None, :, :] < points[:, None, None]

    summed = (field_grid + increment).reshape(stack, band_pairs, 2, outer, INNER)
    north, south = summed[:, :, 0], summed[:, :, 1]
    folded = jnp.stack([north + south, north - south], axis=0)
    folded = jnp.transpose(folded, (2, 3, 0, 1, 4)).reshape(band_pairs, outer, rows, INNER)
    folded = jnp.where(live_cell[:, :, None, :], folded, 0.0)
    folded = folded.reshape(band_pairs, outer * rows, INNER)
    part_cos = jnp.einsum("pyb,pbm->pym", folded, table_cos, precision=high)
    part_neg = jnp.einsum("pyb,pbm->pym", folded, table_neg, precision=high)
    part_cos = part_cos.reshape(band_pairs, outer, rows, wavecount)
    part_neg = part_neg.reshape(band_pairs, outer, rows, wavecount)
    real = jnp.sum(
        ahead_cos[:, :, None, :] * part_cos + ahead_sin[:, :, None, :] * part_neg, axis=1
    )
    imag = jnp.sum(
        ahead_cos[:, :, None, :] * part_neg - ahead_sin[:, :, None, :] * part_cos, axis=1
    )
    spectra = jnp.stack([real, imag], axis=1).reshape(band_pairs * width, wavecount)
    outgoing = spectra.T.reshape(
        band_count * level_groups, 2 * slot_count, band_pairs * width
    )
    arrived = lax.all_to_all(outgoing, ("band", "lev"), split_axis=0, concat_axis=0, tiled=True)
    arrived = arrived.reshape(band_count, level_groups, slot_count, 2, band_pairs, width)
    arrived = jnp.concatenate(
        [arrived[:, level, :, member] for member in range(2) for level in range(level_groups)],
        axis=3,
    )
    arrived = jnp.transpose(arrived, (1, 0, 2, 3))
    lat_count = band_count * band_pairs
    row_width = 2 * level_groups * width
    arrived = arrived.reshape(slot_count, lat_count, row_width)

    own_slots = lax.axis_index(("band", "lev")) * slot_count + lax.iota(jnp.int32, slot_count)
    lower_wave = jnp.take(pair_of_slot, own_slots)
    columns = lax.iota(jnp.int32, wavecount + 1)
    second_member = columns[None, :] >= (wavecount - lower_wave)[:, None]
    degree = jnp.where(second_member, columns[None, :] - 1, lower_wave[:, None] + columns[None, :])
    wave_of_column = jnp.where(
        second_member, wavecount - 1 - lower_wave[:, None], lower_wave[:, None]
    )
    odd = (degree - wave_of_column) % 2
    degree_real = degree.astype(jnp.float32)
    degree_ratio = degree_real * (degree_real + 1.0) / float((wavecount - 1) * wavecount)
    lane = lax.iota(jnp.int32, row_width)
    lane_group = lane // (level_groups * width) * 2 + lane // stack % 2
    column_group = second_member.astype(jnp.int32) * 2 + odd
    own = strength.reshape(fields, level_groups, local_levels)
    rate = jnp.moveaxis(own, 1, 0).reshape(1, level_groups, 1, stack)
    rate = jnp.broadcast_to(rate, (2, level_groups, 4, stack)).reshape(row_width)
    damping = 1.0 / (1.0 + rate[None, None, :] * (degree_ratio * degree_ratio)[:, :, None])
    damping = jnp.where(column_group[:, :, None] == lane_group[None, None, :], damping, 0.0)
    analysed = jnp.einsum("sjc,sjr->scr", legendre, arrived, precision=high)
    returned = jnp.einsum("sjc,scr->sjr", legendre, analysed * damping, precision=high)

    leaving = returned.reshape(slot_count, band_count, band_pairs, 2, level_groups, width)
    leaving = jnp.transpose(leaving, (1, 4, 0, 3, 2, 5)).reshape(
        band_count * level_groups, 2 * slot_count, band_pairs * width
    )
    home = lax.all_to_all(leaving, ("band", "lev"), split_axis=0, concat_axis=0, tiled=True)
    home = home.reshape(wavecount, band_pairs * width).T.reshape(band_pairs, 2, rows, wavecount)
    real, imag = home[:, 0][:, None], home[:, 1][:, None]
    turned_real = real * behind_cos[:, :, None, :] - imag * behind_sin[:, :, None, :]
    turned_imag = real * behind_sin[:, :, None, :] + imag * behind_cos[:, :, None, :]
    turned_real = turned_real.reshape(band_pairs, outer * rows, wavecount)
    turned_imag = turned_imag.reshape(band_pairs, outer * rows, wavecount)
    cells = jnp.einsum("pym,pbm->pyb", turned_real, table_cos, precision=high)
    cells = cells + jnp.einsum("pym,pbm->pyb", turned_imag, table_neg, precision=high)
    cells = cells.reshape(band_pairs, outer, rows, INNER)
    cells = jnp.where(live_cell[:, :, None, :], cells, 0.0)
    cells = cells.reshape(band_pairs, outer, 2, stack, INNER)
    even, uneven = cells[:, :, 0], cells[:, :, 1]
    stepped = jnp.stack([even + uneven, even - uneven], axis=0)
    stepped = jnp.transpose(stepped, (3, 1, 0, 2, 4))
    return stepped.reshape(fields, local_levels, band_pairs, 2, length)


def solution(mesh):
    return jax.shard_map(
        body,
        mesh=mesh,
        in_specs=(
            P(None, "lev", "band", None, None),
            P(None, "lev", "band", None, None),
            P("band"),
            P(),
            P(),
            P(("band", "lev"), None, None),
            P(),
        ),
        out_specs=P(None, "lev", "band", None, None),
        check_vma=False,
    )
```
